32 devices in a mesh: ty: 4 (over x, core), tx: 8 (over z, y).
Axes of the slice: x: 2, y: 2, z: 4, core: 2. Of those that a mesh axis runs over, the one named last changes fastest.
Arguments:
- measured: float32 [4, 8, 32, 128, 128], P('ty', 'tx'), may hold values from 0 to 4
- positions: int32 [4, 8, 32, 2], P('ty', 'tx'), may hold values from 0 to 511, as said below
- owners: int32 [4, 8, 32], P('ty', 'tx'), may hold values from 0 to 31, as said below
- counts: int32 [4, 8], P('ty', 'tx'), may hold values from 16 to 32, as said below
- object_field: float32 [2, 2048, 4096], P(None, 'ty', 'tx'), may hold values from -4 to 4
- probe_field: float32 [2, 128, 128], replicated, may hold values from -6 to 6
Outputs:
- new_object: float32 [2, 2048, 4096], P(None, 'ty', 'tx')
- new_probe: float32 [2, 128, 128], replicated
The draws below stay inside these ranges and needn't reach their ends.
Inputs may be any that keep to these rules, and one draw needn't show every extreme that they name: `positions`: for a live slot the entry is a cell of the owner's tile: row below 512, column below 512; other slots hold arbitrary cells of a tile. The owner of a live slot is the holding device's own tile or one of the up to eight tiles beside it (diagonals included). From one device at most 2 live slots go to any one other tile, and in every draw some tile receives exactly 2 from each of its eight neighbours. Slots that are not live hold arbitrary owners. `counts`: some device is full (32 live slots) in every draw.
All inputs are finite; a program needn't handle non-finite values.
Results may differ from the reference program's by a relative error of at most 0.0003.
Values sent between devices are 32-bit elements; how exact they have to be, the bound alone decides.
No kernel may reach another device: no remote copies, remote signals or barrier semaphores. Data moves between devices by JAX's collectives and lax.ppermute only.
A program may use at most 128 MiB of HBM per device.

```python
import jax
import jax.numpy as jnp
from jax import lax

M = 128
TH = 512
TW = 512
SLOTS = 32
MOVE = 2
NYC = 2048
NXC = 4096
N_TY = 4
N_TX = 8


def tile_layout(key):
    base = jax.random.fold_in(key, 7)
    keys_all = jax.random.split(base, 10)
    devices = N_TY * N_TX
    dev_ids = jnp.arange(devices, dtype=jnp.int32)
    dev_row = (dev_ids // N_TX)[:, None]
    dev_col = (dev_ids % N_TX)[:, None]
    step_rows = jnp.array([-1, -1, -1, 0, 0, 1, 1, 1], dtype=jnp.int32)
    step_cols = jnp.array([-1, 0, 1, -1, 1, -1, 0, 1], dtype=jnp.int32)
    dest_row = dev_row + step_rows[None, :]
    dest_col = dev_col + step_cols[None, :]
    inside = (dest_row >= 0) & (dest_row < N_TY) & (dest_col >= 0) & (dest_col < N_TX)
    hot_row = jax.random.randint(keys_all[0], (), 1, N_TY - 1)
    hot_col = jax.random.randint(keys_all[1], (), 1, N_TX - 1)
    is_hot = (dest_row == hot_row) & (dest_col == hot_col)
    movers = jax.random.randint(keys_all[2], (devices, 8), 0, MOVE + 1)
    movers = jnp.where(is_hot, MOVE, movers) * inside.astype(jnp.int32)
    slot_counts = jax.random.randint(keys_all[3], (devices,), 8 * MOVE, SLOTS + 1)
    fullest = jax.random.randint(keys_all[4], (), 0, devices)
    slot_counts = jnp.where(dev_ids == fullest, SLOTS, slot_counts)
    slot_ids = jnp.arange(SLOTS, dtype=jnp.int32)[None, :]
    scores = jax.random.randint(keys_all[5], (devices, SLOTS), 0, 1 << 16) * SLOTS + slot_ids
    scores = jnp.where(slot_ids < slot_counts[:, None], scores, scores + (1 << 16) * SLOTS)
    ranking = jnp.argsort(jnp.argsort(scores, axis=1), axis=1).astype(jnp.int32)
    bounds = jnp.cumsum(movers, axis=1)
    category = jnp.sum((ranking[:, :, None] >= bounds[:, None, :]).astype(jnp.int32), axis=2)
    moving = category < 8
    capped = jnp.minimum(category, 7)
    row_step = jnp.where(moving, step_rows[capped], 0)
    col_step = jnp.where(moving, step_cols[capped], 0)
    near_row = jax.random.randint(keys_all[6], (devices, SLOTS), 0, M // 2)
    near_col = jax.random.randint(keys_all[7], (devices, SLOTS), 0, M // 2)
    any_row = jax.random.randint(keys_all[8], (devices, SLOTS), 0, TH)
    any_col = jax.random.randint(keys_all[9], (devices, SLOTS), 0, TW)
    pos_row = jnp.where(row_step == -1, TH - 1 - near_row, jnp.where(row_step == 1, near_row, any_row))
    pos_col = jnp.where(col_step == -1, TW - 1 - near_col, jnp.where(col_step == 1, near_col, any_col))
    live_slots = slot_ids < slot_counts[:, None]
    stray_owner = jax.random.randint(jax.random.fold_in(base, 11), (devices, SLOTS), 0, devices)
    owner_ids = jnp.where(live_slots, (dev_row + row_step) * N_TX + dev_col + col_step, stray_owner)
    position_table = jnp.stack([pos_row, pos_col], axis=-1).reshape(N_TY, N_TX, SLOTS, 2).astype(jnp.int32)
    return (position_table, owner_ids.reshape(N_TY, N_TX, SLOTS).astype(jnp.int32), slot_counts.reshape(N_TY, N_TX).astype(jnp.int32))


def draw_positions(key, part):
    return tile_layout(key)[0]


def draw_owners(key, part):
    return tile_layout(key)[1]


def draw_counts(key, part):
    return tile_layout(key)[2]


def steps_of(key, dims, shards, least, largest):
    def one(dim, parts):
        steps = jax.random.uniform(jax.random.fold_in(jax.random.fold_in(key, 6), dim), (parts,), jnp.float32, least / len(shards), largest / len(shards))
        return jnp.repeat(jnp.exp(steps), dims[dim] // parts).reshape((-1,) + (1,) * (len(dims) - dim - 1))

    level = one(*shards[0])
    for cut in shards[1:]:
        level = level * one(*cut)
    return level


def scatter_about(stream_key, dims, deviation, reach, cuts=(), kind=jnp.bfloat16):
    values = deviation * jax.random.normal(stream_key, dims, jnp.float32)
    if cuts:
        values = values * steps_of(stream_key, dims, cuts, -0.22, 0.18)
    return jnp.clip(values, -reach, reach).astype(kind)


def setup_inputs(seed: int = 0) -> dict:
    keys = jax.random.split(jax.random.key(seed), 7)
    measured = jnp.clip(4.0 * jax.random.uniform(keys[0], (N_TY, N_TX, SLOTS, M, M), jnp.float32) ** steps_of(keys[0], (N_TY, N_TX, SLOTS, M, M), ((0, 4), (1, 8)), -0.2, 0.2), 0.0, 4.0)
    positions = draw_positions(jax.random.fold_in(keys[6], 71), 0)
    owners = draw_owners(jax.random.fold_in(keys[6], 71), 0)
    counts = draw_counts(jax.random.fold_in(keys[6], 71), 0)
    object_field = scatter_about(keys[4], (2, NYC, NXC), 0.7, 4.0, ((1, 4), (2, 8)), jnp.float32)
    probe_field = scatter_about(keys[5], (2, M, M), 1.0, 6.0, (), jnp.float32)
    return {"measured": measured, "positions": positions, "owners": owners, "counts": counts, "object_field": object_field, "probe_field": probe_field}


offset_level = 1.0
floor_level = 1.0
tiny_level = 1e-6


def pattern_terms(probe_field, patches, measured_block, live_mask):
    probe_real = probe_field[0]
    probe_imag = probe_field[1]
    patch_real = patches[:, 0]
    patch_imag = patches[:, 1]
    exit_real = probe_real * patch_real - probe_imag * patch_imag
    exit_imag = probe_real * patch_imag + probe_imag * patch_real
    farfield = jnp.fft.fft2(lax.complex(exit_real, exit_imag), norm="ortho")
    far_real = jnp.real(farfield)
    far_imag = jnp.imag(farfield)
    power = far_real * far_real + far_imag * far_imag
    ratio = 1.0 - measured_block / (power + offset_level)
    backward = jnp.fft.ifft2(lax.complex(far_real * ratio, far_imag * ratio), norm="ortho")
    chi_real = jnp.real(backward) * live_mask[:, None, None]
    chi_imag = jnp.imag(backward) * live_mask[:, None, None]
    object_real = probe_real * chi_real + probe_imag * chi_imag
    object_imag = probe_real * chi_imag - probe_imag * chi_real
    lighting = (probe_real * probe_real + probe_imag * probe_imag)[None] * live_mask[:, None, None]
    spread = jnp.stack([object_real, object_imag, lighting], axis=1)
    grad_real = jnp.sum(patch_real * chi_real + patch_imag * chi_imag, axis=0)
    grad_imag = jnp.sum(patch_real * chi_imag - patch_imag * chi_real, axis=0)
    weight = jnp.sum((patch_real * patch_real + patch_imag * patch_imag) * live_mask[:, None, None], axis=0)
    return spread, grad_real, grad_imag, weight


def add_patches(accumulated, spread, start_rows, start_cols):
    zero_index = jnp.zeros((), jnp.int32)

    def add_one(patch_id, current):
        row_start = start_rows[patch_id]
        col_start = start_cols[patch_id]
        window = lax.dynamic_slice(current, (zero_index, row_start, col_start), spread.shape[1:])
        return lax.dynamic_update_slice(current, window + spread[patch_id], (zero_index, row_start, col_start))

    return lax.fori_loop(0, spread.shape[0], add_one, accumulated)


def reference(measured, positions, owners, counts, object_field, probe_field):
    rim_width = M // 2
    tile_rows = object_field.shape[1] // N_TY
    tile_cols = object_field.shape[2] // N_TX
    padded = jnp.pad(object_field, ((0, 0), (rim_width, rim_width), (rim_width, rim_width)))
    devices = N_TY * N_TX
    flat_measured = measured.reshape(devices, SLOTS, M, M)
    flat_positions = positions.reshape(devices, SLOTS, 2).astype(jnp.int32)
    flat_owners = owners.reshape(devices, SLOTS).astype(jnp.int32)
    flat_counts = counts.reshape(devices).astype(jnp.int32)
    slot_ids = jnp.arange(SLOTS, dtype=jnp.int32)
    zero_index = jnp.zeros((), jnp.int32)

    def per_device(state_carry, inputs_now):
        accumulated, grad_real, grad_imag, weight = state_carry
        measured_now, positions_now, owners_now, count_now = inputs_now
        live_mask = (slot_ids < count_now).astype(jnp.float32)
        start_rows = ((owners_now // N_TX) * tile_rows + positions_now[:, 0]).astype(jnp.int32)
        start_cols = ((owners_now % N_TX) * tile_cols + positions_now[:, 1]).astype(jnp.int32)
        patches = jax.vmap(lambda row_start, col_start: lax.dynamic_slice(padded, (zero_index, row_start, col_start), (2, M, M)))(start_rows, start_cols)
        spread, part_real, part_imag, part_weight = pattern_terms(probe_field, patches, measured_now, live_mask)
        accumulated = add_patches(accumulated, spread, start_rows, start_cols)
        return (accumulated, grad_real + part_real, grad_imag + part_imag, weight + part_weight), None

    start_state = (jnp.zeros((3, padded.shape[1], padded.shape[2]), jnp.float32), jnp.zeros((M, M), jnp.float32), jnp.zeros((M, M), jnp.float32), jnp.zeros((M, M), jnp.float32))
    final_state, _ = lax.scan(per_device, start_state, (flat_measured, flat_positions, flat_owners, flat_counts))
    accumulated, grad_real, grad_imag, weight = final_state
    interior = accumulated[:, rim_width:rim_width + object_field.shape[1], rim_width:rim_width + object_field.shape[2]]
    new_object = object_field - interior[:2] / (interior[2] + floor_level)
    new_probe = probe_field - jnp.stack([grad_real, grad_imag]) / (weight + tiny_level)
    return new_object, new_probe
```

```python
import math

import jax
import jax.numpy as jnp
import numpy as np
from jax import lax
from jax.experimental import pallas as pl
from jax.experimental.pallas import tpu as pltpu
from jax.sharding import PartitionSpec as P

M = 128
HALF = M // 2
LANES = 128
MOVE = 2
FLOOR = 1.0
OFFSET = 1.0
TINY = 1e-06
F32 = jnp.float32
BF16 = jnp.bfloat16
I32 = jnp.int32
ROWS_PAD = HALF
TAGS = 4


def dft_blocks():
    index = np.arange(M)
    phase = (np.outer(index, index) % M) * (2.0 * np.pi / M)
    cosine = np.cos(phase) / math.sqrt(M)
    sine = np.sin(phase) / math.sqrt(M)
    right = np.block([[cosine, -sine], [sine, cosine]])
    left = np.block([[cosine, sine], [-sine, cosine]])

    def parts(table):
        high = table.astype(np.float32).astype(BF16)
        low = (table - high.astype(np.float64)).astype(BF16)
        return high, low

    right_high, right_low = parts(right)
    left_high, left_low = parts(left)
    return np.stack([right_high, right_low, left_high, left_low])


def any_spec():
    return pl.BlockSpec(memory_space=pl.ANY)


def vmem_spec():
    return pl.BlockSpec(memory_space=pltpu.VMEM)


def smem_spec():
    return pl.BlockSpec(memory_space=pltpu.SMEM)


def split(value):
    high = value.astype(BF16)
    low = (value - high.astype(F32)).astype(BF16)
    return high, low


def right_multiply(value, high, low):
    value_high, value_low = split(value)
    lhs = jnp.concatenate([value_high, value_low, value_high], axis=1)
    rhs = jnp.concatenate([high, high, low], axis=0)
    return jnp.dot(lhs, rhs, preferred_element_type=F32)


def left_multiply(high, low, value):
    value_high, value_low = split(value)
    lhs = jnp.concatenate([high, high, low], axis=1)
    rhs = jnp.concatenate([value_high, value_low, value_high], axis=0)
    return jnp.dot(lhs, rhs, preferred_element_type=F32)


def lane_ids():
    return lax.broadcasted_iota(I32, (M, LANES), 1)


def pair_step(tables, object_ref, probe_ref, total_ref, probe_total_ref, items):
    right_high, right_low, left_high, left_low = (tables[i] for i in range(4))
    blocks = object_ref.shape[0] // 2
    lanes = lane_ids()
    probe_real, probe_imag = probe_ref[0], probe_ref[1]
    patches = []
    exits = []
    for _, row, col, _ in items:
        block = col // LANES
        shift = col % LANES
        back = (LANES - shift) % LANES
        own = lanes >= shift
        patch = []
        for part in range(2):
            first = object_ref[part * blocks + block, pl.ds(row, M), :]
            second = object_ref[part * blocks + block + 1, pl.ds(row, M), :]
            patch.append(pltpu.roll(jnp.where(own, first, second), back, 1))
        patches.append(patch)
        exits.append(
            jnp.concatenate(
                [
                    probe_real * patch[0] - probe_imag * patch[1],
                    probe_real * patch[1] + probe_imag * patch[0],
                ],
                axis=1,
            )
        )
    half = right_multiply(jnp.concatenate(exits, axis=0), right_high, right_low)
    half = jnp.concatenate(
        [
            jnp.concatenate([half[:M, :M], half[M:, :M]], axis=1),
            jnp.concatenate([half[:M, M:], half[M:, M:]], axis=1),
        ],
        axis=0,
    )
    far = left_multiply(left_high, left_low, half)
    columns = []
    for at, (read, _, _, _) in enumerate(items):
        far_real = far[:M, at * M : (at + 1) * M]
        far_imag = far[M:, at * M : (at + 1) * M]
        power = far_real * far_real + far_imag * far_imag
        ratio = 1.0 - read() / (power + OFFSET)
        columns.append(jnp.concatenate([far_real * ratio, far_imag * ratio], axis=0))
    back_half = left_multiply(right_high, right_low, jnp.concatenate(columns, axis=1))
    back_half = jnp.concatenate(
        [
            jnp.concatenate([back_half[:M, :M], back_half[M:, :M]], axis=1),
            jnp.concatenate([back_half[:M, M:], back_half[M:, M:]], axis=1),
        ],
        axis=0,
    )
    chi = right_multiply(back_half, left_high, left_low)
    sums = [probe_total_ref[i] for i in range(3)]
    for at, (_, row, col, weight) in enumerate(items):
        chi_real = chi[at * M : (at + 1) * M, :M]
        chi_imag = chi[at * M : (at + 1) * M, M:]
        patch_real, patch_imag = patches[at]
        light = patch_real * patch_real + patch_imag * patch_imag
        if weight is not None:
            chi_real = chi_real * weight
            chi_imag = chi_imag * weight
            light = light * weight
        sums[0] += patch_real * chi_real + patch_imag * chi_imag
        sums[1] += patch_real * chi_imag - patch_imag * chi_real
        sums[2] += light
        block = col // LANES
        shift = col % LANES
        own = lanes >= shift
        bright = probe_real * probe_real + probe_imag * probe_imag
        spread = (
            probe_real * chi_real + probe_imag * chi_imag,
            probe_real * chi_imag - probe_imag * chi_real,
            bright if weight is None else bright * weight,
        )
        for part in range(3):
            moved = pltpu.roll(spread[part], shift, 1)
            here = (part * blocks + block, pl.ds(row, M), slice(None))
            after = (part * blocks + block + 1, pl.ds(row, M), slice(None))
            total_ref[here] = total_ref[here] + jnp.where(own, moved, 0.0)
            total_ref[after] = total_ref[after] + jnp.where(own, 0.0, moved)
    for i in range(3):
        probe_total_ref[i] = sums[i]


def run_pairs(count, rows_ref, cols_ref, held_ref, sems, tables, object_ref, probe_ref, total_ref, probe_total_ref):
    def arrived(at):
        pltpu.make_async_copy(held_ref.at[at], held_ref.at[at], sems.at[at]).wait()

    def one_pair(pair, carry):
        first = pair * 2
        paired = first + 1 < count
        second = jnp.where(paired, first + 1, first)
        arrived(first)

        @pl.when(paired)
        def _():
            arrived(second)

        weight = jnp.where(paired, 1.0, 0.0).astype(F32)
        items = [
            (lambda: held_ref[first], rows_ref[first], cols_ref[first], None),
            (lambda: held_ref[second], rows_ref[second], cols_ref[second], weight),
        ]
        pair_step(tables, object_ref, probe_ref, total_ref, probe_total_ref, items)
        return carry

    lax.fori_loop(0, (count + 1) // 2, one_pair, 0)


NEIGHBOURS = [(-1, -1), (-1, 0), (-1, 1), (0, -1), (0, 1), (1, -1), (1, 0), (1, 1)]
TAG_ROWS = 8


def pack_kernel(grid_cols, pos_ref, own_ref, count_ref, measured_ref, object_ref, right_ref, left_ref, up_ref, down_ref, edge_ref, picked_ref, number_ref, sems):
    row_here = lax.axis_index("ty")
    col_here = lax.axis_index("tx")
    rows, cols = object_ref.shape[1], object_ref.shape[2]
    centre = cols // LANES
    copies = []
    for part in range(2):
        copies.append((object_ref.at[part, :, pl.ds(0, LANES)], edge_ref.at[part]))
        copies.append((object_ref.at[part, :, pl.ds(cols - LANES, LANES)], edge_ref.at[2 + part]))
        for block in range(centre):
            at = (part * centre + block) * HALF
            lanes = pl.ds(block * LANES, LANES)
            copies.append((object_ref.at[part, pl.ds(0, HALF), lanes], up_ref.at[pl.ds(at, HALF)]))
            copies.append((object_ref.at[part, pl.ds(rows - HALF, HALF), lanes], down_ref.at[pl.ds(at, HALF)]))
    copies = [pltpu.make_async_copy(src, dst, sems.at[i]) for i, (src, dst) in enumerate(copies)]
    for copy in copies:
        copy.start()
    for way in range(9):
        number_ref[way] = 0
    for way in range(18):
        picked_ref[way] = 0

    def look(slot, carry):
        @pl.when(slot < count_ref[0, 0])
        def _():
            owner = own_ref[0, slot]
            down_step = owner // grid_cols - row_here
            right_step = owner % grid_cols - col_here
            way = (down_step + 1) * 3 + right_step + 1
            have = number_ref[way]

            @pl.when(have < MOVE)
            def _():
                picked_ref[way * MOVE + have] = slot
                number_ref[way] = have + 1

        return carry

    lax.fori_loop(0, own_ref.shape[1], look, 0)
    at_halo = rows
    at_side = 2 * centre * HALF
    plan = []
    for ref, base, ways in (
        (right_ref, at_halo, [(0, 1)]),
        (left_ref, at_halo, [(0, -1)]),
        (up_ref, at_side, [(-1, 0), (-1, 1), (-1, -1)]),
        (down_ref, at_side, [(1, 0), (1, 1), (1, -1)]),
    ):
        lane = lax.broadcasted_iota(I32, (TAG_ROWS, LANES), 1)
        tag = jnp.zeros((TAG_ROWS, LANES), F32)
        for order, (down_step, right_step) in enumerate(ways):
            way = (down_step + 1) * 3 + right_step + 1
            for item in range(MOVE):
                slot = picked_ref[way * MOVE + item]
                place = order * MOVE + item
                plan.append((slot, ref, base + place * M))
                valid = (item < number_ref[way]).astype(I32)
                for offset, value in enumerate((valid, pos_ref[0, 2 * slot], pos_ref[0, 2 * slot + 1])):
                    tag = jnp.where(lane == place * TAGS + offset, value.astype(F32), tag)
        ref[pl.ds(base + len(ways) * MOVE * M, TAG_ROWS), :] = tag
    first = len(copies)
    moves = [
        pltpu.make_async_copy(measured_ref.at[slot], ref.at[pl.ds(at, M)], sems.at[first + i])
        for i, (slot, ref, at) in enumerate(plan)
    ]
    for copy in moves:
        copy.start()
    for copy in copies:
        copy.wait()
    lanes = lax.broadcasted_iota(I32, (rows, LANES), 1)
    low = lanes < HALF
    right_ref[pl.ds(0, rows), :] = jnp.where(low, pltpu.roll(edge_ref[2], HALF, 1), edge_ref[3])
    left_ref[pl.ds(0, rows), :] = jnp.where(low, edge_ref[0], pltpu.roll(edge_ref[1], HALF, 1))
    for copy in moves:
        copy.wait()


def pack(positions, owners, counts, measured, object_field, grid_cols):
    rows, cols = object_field.shape[1], object_field.shape[2]
    centre = cols // LANES
    side = rows + MOVE * M + TAG_ROWS
    tall = 2 * centre * HALF + 3 * MOVE * M + TAG_ROWS
    slots = measured.shape[0]
    return pl.pallas_call(
        lambda *refs: pack_kernel(grid_cols, *refs),
        out_shape=[jax.ShapeDtypeStruct((n, LANES), F32) for n in (side, side, tall, tall)],
        in_specs=[smem_spec(), smem_spec(), smem_spec(), any_spec(), any_spec()],
        out_specs=[vmem_spec()] * 4,
        scratch_shapes=[
            pltpu.VMEM((4, rows, LANES), F32),
            pltpu.SMEM((18,), I32),
            pltpu.SMEM((9,), I32),
            pltpu.SemaphoreType.DMA((4 + 4 * centre + 8 * MOVE,)),
        ],
        name="pack",
        compiler_params=pltpu.CompilerParams(vmem_limit_bytes=8 << 20),
    )(positions.reshape(1, 2 * slots), owners.reshape(1, slots), counts.reshape(1, 1), measured, object_field)


def own_kernel(grid_cols, pos_ref, own_ref, count_ref, measured_ref, object_ref, probe_ref, table_ref, left_ref, right_ref, above_ref, below_ref, above_corner_ref, below_corner_ref, padded_ref, total_ref, probe_total_ref, held_ref, rows_ref, cols_ref, sems, tile_sems):
    row_here = lax.axis_index("ty")
    col_here = lax.axis_index("tx")
    me = row_here * grid_cols + col_here
    rows, cols = object_ref.shape[1], object_ref.shape[2]
    centre = cols // LANES
    blocks = centre + 2
    copies = []
    for part in range(2):
        for block in range(centre):
            here = part * blocks + 1 + block
            copies.append((object_ref.at[part, :, pl.ds(block * LANES, LANES)], padded_ref.at[here, pl.ds(HALF, rows)]))
            at = (part * centre + block) * HALF
            copies.append((above_ref.at[pl.ds(at, HALF)], padded_ref.at[here, pl.ds(0, HALF)]))
            copies.append((below_ref.at[pl.ds(at, HALF)], padded_ref.at[here, pl.ds(HALF + rows, HALF)]))
    copies = [pltpu.make_async_copy(src, dst, tile_sems.at[i]) for i, (src, dst) in enumerate(copies)]
    for copy in copies:
        copy.start()

    def look(slot, number):
        mine = (slot < count_ref[0, 0]) & (own_ref[0, slot] == me)

        @pl.when(mine)
        def _():
            rows_ref[number] = pos_ref[0, 2 * slot]
            cols_ref[number] = pos_ref[0, 2 * slot + 1] + HALF
            pltpu.make_async_copy(measured_ref.at[slot], held_ref.at[number], sems.at[number]).start()

        return number + mine.astype(I32)

    number = lax.fori_loop(0, own_ref.shape[1], look, 0)
    last = blocks - 1
    for start, size, from_left, from_right in (
        (HALF, rows, left_ref[pl.ds(0, rows), :], right_ref[pl.ds(0, rows), :]),
        (0, HALF, above_corner_ref[pl.ds(0, HALF), :], above_corner_ref[pl.ds(HALF, HALF), :]),
        (HALF + rows, HALF, below_corner_ref[pl.ds(0, HALF), :], below_corner_ref[pl.ds(HALF, HALF), :]),
    ):
        span = pl.ds(start, size)
        padded_ref[0, span, :] = pltpu.roll(from_left, HALF, 1)
        padded_ref[blocks, span, :] = from_left
        padded_ref[last, span, :] = from_right
        padded_ref[blocks + last, span, :] = pltpu.roll(from_right, HALF, 1)
    total_ref[...] = jnp.zeros_like(total_ref)
    probe_total_ref[...] = jnp.zeros_like(probe_total_ref)
    for copy in copies:
        copy.wait()
    run_pairs(number, rows_ref, cols_ref, held_ref, sems, table_ref, padded_ref, probe_ref, total_ref, probe_total_ref)


def own_patterns(positions, owners, counts, measured, object_field, probe_field, tables, left, right, above, below, above_corner, below_corner, grid_cols):
    rows, cols = object_field.shape[1], object_field.shape[2]
    centre = cols // LANES
    blocks = centre + 2
    slots = measured.shape[0]
    return pl.pallas_call(
        lambda *refs: own_kernel(grid_cols, *refs),
        out_shape=[
            jax.ShapeDtypeStruct((2 * blocks, rows + M, LANES), F32),
            jax.ShapeDtypeStruct((3 * blocks, rows + M, LANES), F32),
            jax.ShapeDtypeStruct((3, M, M), F32),
        ],
        in_specs=[smem_spec()] * 3 + [any_spec()] * 2 + [vmem_spec()] * 2 + [vmem_spec()] * 2 + [any_spec()] * 2 + [vmem_spec()] * 2,
        out_specs=[vmem_spec()] * 3,
        scratch_shapes=[
            pltpu.VMEM((slots, M, M), F32),
            pltpu.SMEM((slots,), I32),
            pltpu.SMEM((slots,), I32),
            pltpu.SemaphoreType.DMA((slots,)),
            pltpu.SemaphoreType.DMA((6 * centre,)),
        ],
        name="own",
        compiler_params=pltpu.CompilerParams(vmem_limit_bytes=40 << 20),
        cost_estimate=pl.CostEstimate(flops=10**10, bytes_accessed=10**7, transcendentals=0),
    )(positions.reshape(1, 2 * slots), owners.reshape(1, slots), counts.reshape(1, 1), measured, object_field, probe_field, tables, left, right, above, below, above_corner, below_corner)


def moved_kernel(rows, centre, left_ref, right_ref, above_ref, below_ref, left_diag_ref, right_diag_ref, probe_ref, table_ref, padded_ref, total_in, probe_total_in, total_ref, probe_total_ref, up_ref, down_ref, held_ref, tags_ref, rows_ref, cols_ref, sems, tag_sems, total_sem):
    blocks = centre + 2
    side = 2 * centre * HALF
    tag_sources = [
        left_ref.at[pl.ds(rows + MOVE * M, TAG_ROWS)],
        right_ref.at[pl.ds(rows + MOVE * M, TAG_ROWS)],
        above_ref.at[pl.ds(side + 3 * MOVE * M, TAG_ROWS)],
        below_ref.at[pl.ds(side + 3 * MOVE * M, TAG_ROWS)],
        left_diag_ref.at[pl.ds(2 * MOVE * M, TAG_ROWS)],
        left_diag_ref.at[pl.ds(2 * MOVE * M + TAG_ROWS, TAG_ROWS)],
        right_diag_ref.at[pl.ds(2 * MOVE * M, TAG_ROWS)],
        right_diag_ref.at[pl.ds(2 * MOVE * M + TAG_ROWS, TAG_ROWS)],
    ]
    copies = [pltpu.make_async_copy(src, tags_ref.at[i], tag_sems.at[i]) for i, src in enumerate(tag_sources)]
    for copy in copies:
        copy.start()
    big = pltpu.make_async_copy(total_in, total_ref, total_sem)
    big.start()
    probe_total_ref[...] = probe_total_in[...]
    for copy in copies:
        copy.wait()
    sources = [
        (left_ref, rows, 0, 0),
        (right_ref, rows, 1, 0),
        (above_ref, side, 2, 0),
        (below_ref, side, 3, 0),
        (left_diag_ref, 0, 4, MOVE),
        (left_diag_ref, MOVE * M, 5, MOVE),
        (right_diag_ref, 0, 6, 2 * MOVE),
        (right_diag_ref, MOVE * M, 7, 2 * MOVE),
    ]
    number = jnp.zeros((), I32)
    for ref, base, tag, place in sources:
        for item in range(MOVE):
            at = (place + item) * TAGS
            valid = tags_ref[tag, 0, at].astype(I32)

            @pl.when(valid > 0)
            def _():
                rows_ref[number] = tags_ref[tag, 0, at + 1].astype(I32)
                cols_ref[number] = tags_ref[tag, 0, at + 2].astype(I32) + HALF
                pltpu.make_async_copy(ref.at[pl.ds(base + item * M, M)], held_ref.at[number], sems.at[number]).start()

            number = number + valid
    big.wait()
    run_pairs(number, rows_ref, cols_ref, held_ref, sems, table_ref, padded_ref, probe_ref, total_ref, probe_total_ref)
    last = blocks - 1
    low = lax.broadcasted_iota(I32, (HALF, LANES), 1) < HALF
    for ref, start in ((up_ref, 0), (down_ref, HALF + rows)):
        span = pl.ds(start, HALF)
        for part in range(3):
            for block in range(centre):
                ref[pl.ds((part * centre + block) * HALF, HALF), :] = total_ref[part * blocks + 1 + block, span, :]
        at = 3 * centre * HALF
        ref[pl.ds(at, HALF), :] = jnp.where(low, pltpu.roll(total_ref[0, span, :], HALF, 1), total_ref[blocks, span, :])
        ref[pl.ds(at + HALF, HALF), :] = jnp.where(low, total_ref[last, span, :], pltpu.roll(total_ref[blocks + last, span, :], HALF, 1))
        ref[pl.ds(at + 2 * HALF, HALF), :] = jnp.where(low, total_ref[2 * blocks + last, span, :], total_ref[2 * blocks, span, :])


def moved_patterns(left, right, above, below, left_diag, right_diag, probe_field, tables, padded, total, probe_total, rows, centre):
    blocks = centre + 2
    rim = (3 * centre + 3) * HALF
    return pl.pallas_call(
        lambda *refs: moved_kernel(rows, centre, *refs),
        out_shape=[
            jax.ShapeDtypeStruct(total.shape, F32),
            jax.ShapeDtypeStruct(probe_total.shape, F32),
            jax.ShapeDtypeStruct((rim, LANES), F32),
            jax.ShapeDtypeStruct((rim, LANES), F32),
        ],
        in_specs=[any_spec()] * 6 + [vmem_spec()] * 3 + [any_spec(), vmem_spec()],
        out_specs=[vmem_spec()] * 4,
        scratch_shapes=[
            pltpu.VMEM((8 * MOVE, M, M), F32),
            pltpu.SMEM((8, TAG_ROWS, LANES), F32),
            pltpu.SMEM((8 * MOVE,), I32),
            pltpu.SMEM((8 * MOVE,), I32),
            pltpu.SemaphoreType.DMA((8 * MOVE,)),
            pltpu.SemaphoreType.DMA((8,)),
            pltpu.SemaphoreType.DMA,
        ],
        name="moved",
        compiler_params=pltpu.CompilerParams(vmem_limit_bytes=40 << 20),
        cost_estimate=pl.CostEstimate(flops=5 * 10**9, bytes_accessed=10**7, transcendentals=0),
    )(left, right, above, below, left_diag, right_diag, probe_field, tables, padded, total, probe_total)


def side_kernel(rows, centre, total_ref, above_ref, below_ref, left_ref, right_ref, edge_ref, corner_ref, sems):
    blocks = centre + 2
    last = blocks - 1
    at = 3 * centre * HALF
    copies = []
    for part in range(3):
        for edge, block in enumerate((0, last)):
            copies.append((total_ref.at[part * blocks + block, pl.ds(HALF, rows)], edge_ref.at[part * 2 + edge]))
    copies.append((above_ref.at[pl.ds(at, 3 * HALF)], corner_ref.at[0]))
    copies.append((below_ref.at[pl.ds(at, 3 * HALF)], corner_ref.at[1]))
    copies = [pltpu.make_async_copy(src, dst, sems.at[i]) for i, (src, dst) in enumerate(copies)]
    for copy in copies:
        copy.start()
    for copy in copies:
        copy.wait()
    low = lax.broadcasted_iota(I32, (rows, LANES), 1) < HALF
    left_ref[pl.ds(0, rows), :] = jnp.where(low, pltpu.roll(edge_ref[0], HALF, 1), edge_ref[2])
    right_ref[pl.ds(0, rows), :] = jnp.where(low, edge_ref[1], pltpu.roll(edge_ref[3], HALF, 1))
    half = rows // 2
    low = lax.broadcasted_iota(I32, (half, LANES), 1) < HALF
    low_corner = lax.broadcasted_iota(I32, (HALF, LANES), 1) < HALF
    for edge, ref in ((0, left_ref), (1, right_ref)):
        for which, start in ((0, 0), (1, rows - HALF)):
            span = pl.ds(start, HALF)
            ref[span, :] = ref[span, :] + corner_ref[which, pl.ds(edge * HALF, HALF), :]
            keep = low_corner if edge == 1 else ~low_corner
            light = jnp.where(keep, corner_ref[which, pl.ds(2 * HALF, HALF), :], 0.0)
            edge_ref[4 + edge, span, :] = edge_ref[4 + edge, span, :] + light
    left_ref[pl.ds(rows, half), :] = jnp.where(low, pltpu.roll(edge_ref[4, pl.ds(0, half), :], HALF, 1), edge_ref[4, pl.ds(half, half), :])
    right_ref[pl.ds(rows, half), :] = jnp.where(low, edge_ref[5, pl.ds(0, half), :], pltpu.roll(edge_ref[5, pl.ds(half, half), :], HALF, 1))


def side_rims(total, above, below, rows, centre):
    tall = rows + rows // 2
    return pl.pallas_call(
        lambda *refs: side_kernel(rows, centre, *refs),
        out_shape=[jax.ShapeDtypeStruct((tall, LANES), F32)] * 2,
        in_specs=[any_spec()] * 3,
        out_specs=[vmem_spec()] * 2,
        scratch_shapes=[
            pltpu.VMEM((6, rows, LANES), F32),
            pltpu.VMEM((2, 3 * HALF, LANES), F32),
            pltpu.SemaphoreType.DMA((8,)),
        ],
        name="side",
        compiler_params=pltpu.CompilerParams(vmem_limit_bytes=8 << 20),
    )(total, above, below)


def final_kernel(rows, centre, object_ref, total_ref, above_ref, below_ref, left_ref, right_ref, out_ref, sum_ref):
    blocks = centre + 2
    half = rows // 2
    low = lax.broadcasted_iota(I32, (rows, LANES), 1) < HALF
    low_half = lax.broadcasted_iota(I32, (half, LANES), 1) < HALF
    for block in range(centre):
        for part in range(3):
            value = total_ref[part * blocks + 1 + block, pl.ds(HALF, rows), :]
            sum_ref[part] = value
            at = (part * centre + block) * HALF
            sum_ref[part, pl.ds(0, HALF), :] += above_ref[pl.ds(at, HALF), :]
            sum_ref[part, pl.ds(rows - HALF, HALF), :] += below_ref[pl.ds(at, HALF), :]
        if block == 0:
            message = left_ref[pl.ds(0, rows), :]
            sum_ref[0] += jnp.where(low, message, 0.0)
            sum_ref[1] += jnp.where(low, pltpu.roll(message, HALF, 1), 0.0)
            light = left_ref[pl.ds(rows, half), :]
            sum_ref[2, pl.ds(0, half), :] += jnp.where(low_half, light, 0.0)
            sum_ref[2, pl.ds(half, half), :] += jnp.where(low_half, pltpu.roll(light, HALF, 1), 0.0)
        if block == centre - 1:
            message = right_ref[pl.ds(0, rows), :]
            sum_ref[0] += jnp.where(low, 0.0, pltpu.roll(message, HALF, 1))
            sum_ref[1] += jnp.where(low, 0.0, message)
            light = right_ref[pl.ds(rows, half), :]
            sum_ref[2, pl.ds(0, half), :] += jnp.where(low_half, 0.0, pltpu.roll(light, HALF, 1))
            sum_ref[2, pl.ds(half, half), :] += jnp.where(low_half, 0.0, light)
        weight = 1.0 / (sum_ref[2] + FLOOR)
        lanes = pl.ds(block * LANES, LANES)
        for part in range(2):
            out_ref[part, :, lanes] = object_ref[part, :, lanes] - sum_ref[part] * weight


def finish(object_field, total, above, below, left, right, rows, centre):
    return pl.pallas_call(
        lambda *refs: final_kernel(rows, centre, *refs),
        out_shape=jax.ShapeDtypeStruct(object_field.shape, F32),
        in_specs=[vmem_spec()] * 6,
        out_specs=vmem_spec(),
        scratch_shapes=[pltpu.VMEM((3, rows, LANES), F32)],
        name="finish",
        compiler_params=pltpu.CompilerParams(vmem_limit_bytes=40 << 20),
    )(object_field, total, above, below, left, right)


def shift(block, axis, distance):
    devices = lax.axis_size(axis)
    return lax.ppermute(block, axis, [(i, i + distance) for i in range(devices) if 0 <= i + distance < devices])


def swap(block, axis, step):
    return lax.ppermute(block, axis, [(i, i ^ step) for i in range(lax.axis_size(axis))])


def sum_all(value):
    sizes = {axis: lax.axis_size(axis) for axis in ("ty", "tx")}
    if any(size & (size - 1) for size in sizes.values()) or sizes["ty"] < 2:
        return lax.psum(value, ("ty", "tx"))
    shape = value.shape
    halves = value.reshape(2, -1, LANES)
    odd = lax.axis_index("ty") % 2
    kept = jnp.where(odd == 0, halves[0], halves[1])
    given = jnp.where(odd == 0, halves[1], halves[0])
    kept = kept + swap(given, "ty", 1)
    for axis in ("ty", "tx"):
        step = 2 if axis == "ty" else 1
        while step < sizes[axis]:
            kept = kept + swap(kept, axis, step)
            step *= 2
    other = swap(kept, "ty", 1)
    first = jnp.where(odd == 0, kept, other)
    second = jnp.where(odd == 0, other, kept)
    return jnp.stack([first, second]).reshape(shape)


def shards(measured, positions, owners, counts, object_field, probe_field):
    rows, cols = object_field.shape[1], object_field.shape[2]
    centre = cols // LANES
    grid_cols = lax.axis_size("tx")
    measured = measured[0, 0]
    tables = jnp.asarray(dft_blocks())
    to_right, to_left, to_up, to_down = pack(positions, owners, counts, measured, object_field, grid_cols)
    left = shift(to_right, "tx", 1)
    right = shift(to_left, "tx", -1)
    below = shift(to_up, "ty", -1)
    above = shift(to_down, "ty", 1)
    side = 2 * centre * HALF
    tag_at = side + 3 * MOVE * M

    def relay(order):
        span = slice(side + order * MOVE * M, side + (order + 1) * MOVE * M)
        tags = slice(tag_at, tag_at + TAG_ROWS)
        return jnp.concatenate([above[span], below[span], above[tags], below[tags]], axis=0)

    left_diag = shift(relay(1), "tx", 1)
    right_diag = shift(relay(2), "tx", -1)
    below_corner = shift(jnp.concatenate([left[:HALF], right[:HALF]], axis=0), "ty", -1)
    above_corner = shift(jnp.concatenate([left[rows - HALF : rows], right[rows - HALF : rows]], axis=0), "ty", 1)
    padded, total, probe_total = own_patterns(
        positions, owners, counts, measured, object_field, probe_field, tables,
        left, right, above, below, above_corner, below_corner, grid_cols,
    )
    total, probe_total, rim_up, rim_down = moved_patterns(
        left, right, above, below, left_diag, right_diag, probe_field, tables,
        padded, total, probe_total, rows, centre,
    )
    rim_below = shift(rim_up, "ty", -1)
    rim_above = shift(rim_down, "ty", 1)
    rim_left, rim_right = side_rims(total, rim_above, rim_below, rows, centre)
    from_right = shift(rim_left, "tx", -1)
    from_left = shift(rim_right, "tx", 1)
    new_object = finish(object_field, total, rim_above, rim_below, from_left, from_right, rows, centre)
    summed = sum_all(probe_total)
    new_probe = probe_field - summed[:2] / (summed[2] + TINY)
    return new_object, new_probe


def solution(mesh):
    placed = (
        P("ty", "tx", None, None, None),
        P("ty", "tx", None, None),
        P("ty", "tx", None),
        P("ty", "tx"),
        P(None, "ty", "tx"),
        P(),
    )
    return jax.shard_map(
        shards, mesh=mesh, in_specs=placed, out_specs=(P(None, "ty", "tx"), P()), check_vma=False
    )
```

```python
import math

import jax
import jax.numpy as jnp
import numpy as np
from jax import lax
from jax.experimental import pallas as pl
from jax.experimental.pallas import tpu as pltpu
from jax.sharding import PartitionSpec as P


M = 128
HALF = M // 2
LANES = 128
MOVE = 2
FLOOR = 1.0
OFFSET = 1.0
TINY = 1e-06
F32 = jnp.float32
BF16 = jnp.bfloat16
I32 = jnp.int32
TAGS = 4


def dft_blocks():
    index = np.arange(M)
    phase = (np.outer(index, index) % M) * (2.0 * np.pi / M)
    cosine = np.cos(phase) / math.sqrt(M)
    sine = np.sin(phase) / math.sqrt(M)
    right = np.block([[cosine, -sine], [sine, cosine]])
    left = np.block([[cosine, sine], [-sine, cosine]])

    def parts(table):
        high = table.astype(np.float32).astype(BF16)
        low = (table - high.astype(np.float64)).astype(BF16)
        return high, low

    right_high, right_low = parts(right)
    left_high, left_low = parts(left)
    return np.stack([right_high, right_low, left_high, left_low])


def vmem_spec():
    return pl.BlockSpec(memory_space=pltpu.VMEM)


def hbm_spec():
    return pl.BlockSpec(memory_space=pltpu.HBM)


def smem_spec():
    return pl.BlockSpec(memory_space=pltpu.SMEM)


def split(value):
    high = value.astype(BF16)
    low = (value - high.astype(F32)).astype(BF16)
    return high, low


def right_multiply(value, high, low):
    value_high, value_low = split(value)
    lhs = jnp.concatenate([value_high, value_low, value_high], axis=1)
    rhs = jnp.concatenate([high, high, low], axis=0)
    return jnp.dot(lhs, rhs, preferred_element_type=F32)


def left_multiply(high, low, value):
    value_high, value_low = split(value)
    lhs = jnp.concatenate([high, high, low], axis=1)
    rhs = jnp.concatenate([value_high, value_low, value_high], axis=0)
    return jnp.dot(lhs, rhs, preferred_element_type=F32)


def lane_ids():
    return lax.broadcasted_iota(I32, (M, LANES), 1)


def window(ref, index, row, col, lanes):
    block = col // LANES
    shift = col % LANES
    back = (LANES - shift) % LANES
    first = ref[index + block, pl.ds(row, M), :]
    second = ref[index + block + 1, pl.ds(row, M), :]
    return pltpu.roll(jnp.where(lanes >= shift, first, second), back, 1)


def add_window(ref, index, row, col, value, lanes):
    block = col // LANES
    shift = col % LANES
    own = lanes >= shift
    moved = pltpu.roll(value, shift, 1)
    here = ref.at[index + block, pl.ds(row, M), :]
    after = ref.at[index + block + 1, pl.ds(row, M), :]
    pltpu.store(here, here[...] + moved, mask=own)
    pltpu.store(after, after[...] + moved, mask=~own)


def forward_step(tables, object_ref, probe_ref, patch_ref, first, items):
    right_high, right_low, left_high, left_low = (tables[i] for i in range(4))
    blocks = object_ref.shape[0] // 2
    lanes = lane_ids()
    probe_real, probe_imag = probe_ref[0], probe_ref[1]
    exits = []
    for at, (_, row, col, _) in enumerate(items):
        real = window(object_ref, 0, row, col, lanes)
        imag = window(object_ref, blocks, row, col, lanes)
        patch_ref[2 * (first + at)] = real
        patch_ref[2 * (first + at) + 1] = imag
        exits.append(
            jnp.concatenate(
                [probe_real * real - probe_imag * imag, probe_real * imag + probe_imag * real],
                axis=1,
            )
        )
    return exits


def side_by_side(half, count):
    return jnp.concatenate(
        [
            jnp.concatenate([half[M * i : M * (i + 1), part * M : (part + 1) * M] for i in range(count)], axis=1)
            for part in range(2)
        ],
        axis=0,
    )


def stacked(half, count):
    return jnp.concatenate(
        [
            jnp.concatenate([half[part * M : (part + 1) * M, M * i : M * (i + 1)] for part in range(2)], axis=1)
            for i in range(count)
        ],
        axis=0,
    )


def ratio_step(far, items):
    columns = []
    for at, (read, _, _, _) in enumerate(items):
        far_real = far[:M, at * M : (at + 1) * M]
        far_imag = far[M:, at * M : (at + 1) * M]
        power = far_real * far_real + far_imag * far_imag
        ratio = 1.0 - read() / (power + OFFSET)
        columns.append(jnp.concatenate([far_real * ratio, far_imag * ratio], axis=0))
    return jnp.concatenate(columns, axis=1)


def update_step(chi, blocks, bright_ref, probe_ref, patch_ref, first, total_ref, probe_total_ref, items):
    lanes = lane_ids()
    probe_real, probe_imag = probe_ref[0], probe_ref[1]
    sums = [probe_total_ref[i] for i in range(3)]
    for at, (_, row, col, weight) in enumerate(items):
        chi_real = chi[at * M : (at + 1) * M, :M]
        chi_imag = chi[at * M : (at + 1) * M, M:]
        real = patch_ref[2 * (first + at)]
        imag = patch_ref[2 * (first + at) + 1]
        light = real * real + imag * imag
        bright = bright_ref[...]
        if weight is not None:
            chi_real = chi_real * weight
            chi_imag = chi_imag * weight
            light = light * weight
            bright = bright * weight
        sums[0] += real * chi_real + imag * chi_imag
        sums[1] += real * chi_imag - imag * chi_real
        sums[2] += light
        add_window(total_ref, 0, row, col, probe_real * chi_real + probe_imag * chi_imag, lanes)
        add_window(total_ref, blocks, row, col, probe_real * chi_imag - probe_imag * chi_real, lanes)
        add_window(total_ref, 2 * blocks, row, col, bright, lanes)
    for i in range(3):
        probe_total_ref[i] = sums[i]


GROUP = 4


def run_pairs(count, patch_ref, bright_ref, rows_ref, cols_ref, held_ref, sems, tables, object_ref, probe_ref, total_ref, probe_total_ref):
    bright_ref[...] = probe_ref[0] * probe_ref[0] + probe_ref[1] * probe_ref[1]

    def arrived(at):
        pltpu.make_async_copy(held_ref.at[at], held_ref.at[at], sems.at[at]).wait()

    def reader(at):
        return lambda: held_ref[at]

    def one_group(group, carry):
        first = group * GROUP
        items = [(reader(first), rows_ref[first], cols_ref[first], None)]
        arrived(first)
        for i in range(1, GROUP):
            there = first + i < count
            at = jnp.where(there, first + i, first)

            @pl.when(there)
            def _():
                arrived(at)

            items.append((reader(at), rows_ref[at], cols_ref[at], jnp.where(there, 1.0, 0.0).astype(F32)))
        pairs = [items[i : i + 2] for i in range(0, GROUP, 2)]
        exits = [forward_step(tables, object_ref, probe_ref, patch_ref, 2 * i, pair) for i, pair in enumerate(pairs)]
        half = right_multiply(jnp.concatenate(sum(exits, []), axis=0), tables[0], tables[1])
        far = left_multiply(tables[2], tables[3], side_by_side(half, GROUP))
        scaled = ratio_step(far, items)
        half = left_multiply(tables[0], tables[1], scaled)
        chi = right_multiply(stacked(half, GROUP), tables[2], tables[3])
        chis = [chi[2 * M * i : 2 * M * (i + 1)] for i in range(len(pairs))]
        for i, (chi, pair) in enumerate(zip(chis, pairs)):
            update_step(chi, object_ref.shape[0] // 2, bright_ref, probe_ref, patch_ref, 2 * i, total_ref, probe_total_ref, pair)
        return carry

    lax.fori_loop(0, (count + GROUP - 1) // GROUP, one_group, 0)


TAG_ROWS = 8
PACK_VMEM = 16 << 20


def direction(which):
    row_sign = 1 - 2 * (lax.axis_index("ty") % 2)
    col_sign = 1 - 2 * (lax.axis_index("tx") % 2)
    zero = jnp.zeros((), I32)
    return (
        (zero, col_sign),
        (zero, -col_sign),
        (row_sign, zero),
        (-row_sign, zero),
    )[which]


def exchange(block, which):
    size_y, size_x = lax.axis_size("ty"), lax.axis_size("tx")
    pairs = []
    for i in range(size_y):
        for j in range(size_x):
            row_sign, col_sign = 1 - 2 * (i % 2), 1 - 2 * (j % 2)
            down, right = (
                (0, col_sign),
                (0, -col_sign),
                (row_sign, 0),
                (-row_sign, 0),
            )[which]
            if 0 <= i + down < size_y and 0 <= j + right < size_x:
                pairs.append((i * size_x + j, (i + down) * size_x + j + right))
    return lax.ppermute(block, ("ty", "tx"), pairs)


def pack_kernel(grid_cols, pos_ref, own_ref, count_ref, measured_ref, object_ref, *rest):
    out_refs = rest[:4]
    edge_ref, picked_ref, number_ref, edge_sems, strip_sems, sems = rest[4:]
    row_here = lax.axis_index("ty")
    col_here = lax.axis_index("tx")
    rows, cols = object_ref.shape[1], object_ref.shape[2]
    centre = cols // LANES
    edges = []
    for part in range(2):
        edges.append((object_ref.at[part, :, pl.ds(0, LANES)], edge_ref.at[part]))
        edges.append((object_ref.at[part, :, pl.ds(cols - LANES, LANES)], edge_ref.at[2 + part]))
    edges = [pltpu.make_async_copy(src, dst, edge_sems.at[i]) for i, (src, dst) in enumerate(edges)]
    for copy in edges:
        copy.start()
    strips = []
    for which in (2, 3):
        down_step, _ = direction(which)
        start = pl.multiple_of(jnp.where(down_step == 1, rows - HALF, 0), HALF)
        for part in range(2):
            for block in range(centre):
                at = (part * centre + block) * HALF
                src = object_ref.at[part, pl.ds(start, HALF), pl.ds(block * LANES, LANES)]
                strips.append((src, out_refs[which].at[pl.ds(at, HALF)]))
    strips = [pltpu.make_async_copy(src, dst, strip_sems.at[i]) for i, (src, dst) in enumerate(strips)]
    for copy in strips:
        copy.start()
    for way in range(9):
        number_ref[way] = 0
    for way in range(9 * MOVE):
        picked_ref[way] = 0

    def look(slot, carry):
        owner = own_ref[0, 0, slot]
        way = (owner // grid_cols - row_here + 1) * 3 + owner % grid_cols - col_here + 1
        way = jnp.clip(way, 0, 8)
        have = number_ref[way]

        @pl.when((slot < count_ref[0, 0]) & (have < MOVE))
        def _():
            picked_ref[way * MOVE + have] = slot
            number_ref[way] = have + 1

        return carry

    lax.fori_loop(0, own_ref.shape[2], look, 0)
    moves = []
    for which, ref in enumerate(out_refs):
        base = pattern_base(which, rows, centre)
        down_step, right_step = direction(which)
        steps = [right_step] if which < 2 else [0, 1, -1]
        lane = lax.broadcasted_iota(I32, (TAG_ROWS, LANES), 1)
        tag = jnp.zeros((TAG_ROWS, LANES), F32)
        for order, step in enumerate(steps):
            way = (down_step + 1) * 3 + step + 1
            for item in range(MOVE):
                slot = picked_ref[way * MOVE + item]
                place = order * MOVE + item
                move = pltpu.make_async_copy(
                    measured_ref.at[slot], ref.at[pl.ds(base + place * M, M)], sems.at[len(moves)]
                )
                move.start()
                moves.append(move)
                valid = (item < number_ref[way]).astype(I32)
                for offset, value in enumerate((valid, pos_ref[0, 0, slot, 0], pos_ref[0, 0, slot, 1])):
                    tag = jnp.where(lane == place * TAGS + offset, value.astype(F32), tag)
        ref[pl.ds(base + len(steps) * MOVE * M, TAG_ROWS), :] = tag
    for copy in edges:
        copy.wait()
    low = lax.broadcasted_iota(I32, (rows, LANES), 1) < HALF
    for which in (0, 1):
        _, right_step = direction(which)

        @pl.when(right_step == 1)
        def _():
            out_refs[which][pl.ds(0, rows), :] = jnp.where(low, pltpu.roll(edge_ref[2], HALF, 1), edge_ref[3])

        @pl.when(right_step == -1)
        def _():
            out_refs[which][pl.ds(0, rows), :] = jnp.where(low, edge_ref[0], pltpu.roll(edge_ref[1], HALF, 1))

    for copy in strips:
        copy.wait()
    for copy in moves:
        copy.wait()


def pattern_base(which, rows, centre):
    return rows if which < 2 else 2 * centre * HALF


def tag_base(which, rows, centre):
    return pattern_base(which, rows, centre) + (1 if which < 2 else 3) * MOVE * M


RELAY_TAGS = 2 * HALF + 2 * MOVE * M
RELAY_ROWS = RELAY_TAGS + 2 * TAG_ROWS


def relay_kernel(centre, first_ref, second_ref, even_ref, odd_ref):
    side = 2 * centre * HALF
    low = lax.broadcasted_iota(I32, (HALF, LANES), 1) < HALF
    for which, out_ref in ((0, even_ref), (1, odd_ref)):
        _, right_step = direction(which)
        rightward = right_step == 1
        block = jnp.where(rightward, centre - 1, 0)
        start = pl.multiple_of(side + jnp.where(rightward, 1, 2) * MOVE * M, M)
        for slot, ref in enumerate((first_ref, second_ref)):
            real = ref[pl.ds(pl.multiple_of(block * HALF, HALF), HALF), :]
            imag = ref[pl.ds(pl.multiple_of((centre + block) * HALF, HALF), HALF), :]
            span = pl.ds(slot * HALF, HALF)
            shifted = jnp.where(rightward, real, imag)
            stays = jnp.where(rightward, imag, real)
            out_ref[span, :] = jnp.where(low == rightward, pltpu.roll(shifted, HALF, 1), stays)
            out_ref[pl.ds(2 * HALF + slot * MOVE * M, MOVE * M), :] = ref[pl.ds(start, MOVE * M), :]
            out_ref[pl.ds(RELAY_TAGS + slot * TAG_ROWS, TAG_ROWS), :] = ref[pl.ds(side + 3 * MOVE * M, TAG_ROWS), :]


def relay(first, second, centre):
    return pl.pallas_call(
        lambda *refs: relay_kernel(centre, *refs),
        out_shape=[jax.ShapeDtypeStruct((RELAY_ROWS, LANES), F32)] * 2,
        in_specs=[vmem_spec()] * 2,
        out_specs=[vmem_spec()] * 2,
        name="relay",
        compiler_params=pltpu.CompilerParams(vmem_limit_bytes=6 << 20),
    )(first, second)


def pack(scalars, measured, object_field, grid_cols):
    rows, cols = object_field.shape[1], object_field.shape[2]
    centre = cols // LANES
    return pl.pallas_call(
        lambda *refs: pack_kernel(grid_cols, *refs),
        out_shape=[jax.ShapeDtypeStruct((tag_base(which, rows, centre) + TAG_ROWS, LANES), F32) for which in range(4)],
        in_specs=[smem_spec()] * 3 + [hbm_spec()] * 2,
        out_specs=[vmem_spec()] * 4,
        scratch_shapes=[
            pltpu.VMEM((4, rows, LANES), F32),
            pltpu.SMEM((9 * MOVE,), I32),
            pltpu.SMEM((9,), I32),
            pltpu.SemaphoreType.DMA((4,)),
            pltpu.SemaphoreType.DMA((4 * centre,)),
            pltpu.SemaphoreType.DMA((8 * MOVE,)),
        ],
        name="pack",
        compiler_params=pltpu.CompilerParams(vmem_limit_bytes=PACK_VMEM),
    )(*scalars, measured, object_field)


def at_corner(row, col, rows, cols):
    return ((row < HALF) | (row > rows - HALF)) & ((col < HALF) | (col > cols - HALF))


def inside(row, col, rows, cols):
    return (row >= HALF) & (row <= rows - HALF) & (col >= HALF) & (col <= cols - HALF)


INNER, EDGE, CORNER = 0, 1, 2


def place_of(row, col, rows, cols):
    return jnp.where(inside(row, col, rows, cols), INNER, jnp.where(at_corner(row, col, rows, cols), CORNER, EDGE))


def own_list(number, want, grid_cols, rows, cols, pos_ref, own_ref, count_ref, measured_ref, held_ref, rows_ref, cols_ref, sems):
    me = lax.axis_index("ty") * grid_cols + lax.axis_index("tx")

    def look(slot, number):
        row, col = pos_ref[0, 0, slot, 0], pos_ref[0, 0, slot, 1]
        mine = (slot < count_ref[0, 0]) & (own_ref[0, 0, slot] == me)
        mine = mine & (place_of(row, col, rows, cols) == want)

        @pl.when(mine)
        def _():
            rows_ref[number] = row
            cols_ref[number] = col + HALF
            pltpu.make_async_copy(measured_ref.at[slot], held_ref.at[number], sems.at[number]).start()

        return number + mine.astype(I32)

    return lax.fori_loop(0, own_ref.shape[2], look, number)


def moved_list(number, want_corner, rows, cols, arrivals, tags_ref, held_ref, rows_ref, cols_ref, sems):
    for ref, base, tag, order in arrivals:
        for item in range(MOVE):
            at = (order * MOVE + item) * TAGS
            valid = tags_ref[tag, 0, at].astype(I32) > 0
            row = tags_ref[tag, 0, at + 1].astype(I32)
            col = tags_ref[tag, 0, at + 2].astype(I32)
            if want_corner is not None:
                valid = valid & (at_corner(row, col, rows, cols) == want_corner)

            @pl.when(valid)
            def _():
                rows_ref[number] = row
                cols_ref[number] = col + HALF
                pltpu.make_async_copy(ref.at[pl.ds(base + item * M, M)], held_ref.at[number], sems.at[number]).start()

            number = number + valid.astype(I32)
    return number


def put_side(padded_ref, blocks, from_right, span, value):
    rolled = pltpu.roll(value, HALF, 1)
    block = jnp.where(from_right, blocks - 1, 0)
    padded_ref[block, span, :] = jnp.where(from_right, value, rolled)
    padded_ref[blocks + block, span, :] = jnp.where(from_right, rolled, value)


def copy_planes(source_ref, target_ref):
    def one(index, carry):
        target_ref[index] = source_ref[index]
        return carry

    lax.fori_loop(0, target_ref.shape[0], one, 0)


def read_tags(sources, tags_ref, tag_sems):
    copies = [pltpu.make_async_copy(src, tags_ref.at[i], tag_sems.at[i]) for i, src in enumerate(sources)]
    for copy in copies:
        copy.start()
    return copies


def side_tags(sides, rows, centre):
    return [ref.at[pl.ds(tag_base(which, rows, centre), TAG_ROWS)] for which, ref in enumerate(sides)]


def start_tiles(object_ref, padded_ref, tile_sems):
    rows, cols = object_ref.shape[1], object_ref.shape[2]
    centre = cols // LANES
    tiles = []
    for part in range(2):
        for block in range(centre):
            here = part * (centre + 2) + 1 + block
            tiles.append((object_ref.at[part, :, pl.ds(block * LANES, LANES)], padded_ref.at[here, pl.ds(HALF, rows)]))
    tiles = [pltpu.make_async_copy(src, dst, tile_sems.at[i]) for i, (src, dst) in enumerate(tiles)]
    for copy in tiles:
        copy.start()
    return tiles


def inner_kernel(grid_cols, pos_ref, own_ref, count_ref, measured_ref, object_ref, probe_ref, table_ref, *rest):
    total_ref, probe_total_ref = rest[:2]
    padded_ref, held_ref, patch_ref, bright_ref, rows_ref, cols_ref, sems, tile_sems = rest[2:]
    rows, cols = object_ref.shape[1], object_ref.shape[2]
    tiles = start_tiles(object_ref, padded_ref, tile_sems)
    number = own_list(
        jnp.zeros((), I32), INNER, grid_cols, rows, cols, pos_ref, own_ref, count_ref, measured_ref, held_ref, rows_ref, cols_ref, sems
    )
    clear_planes(total_ref)
    probe_total_ref[...] = jnp.zeros_like(probe_total_ref)
    for copy in tiles:
        copy.wait()
    run_pairs(number, patch_ref, bright_ref, rows_ref, cols_ref, held_ref, sems, table_ref, padded_ref, probe_ref, total_ref, probe_total_ref)


def clear_planes(target_ref):
    def one(index, carry):
        target_ref[index] = jnp.zeros(target_ref.shape[1:], F32)
        return carry

    lax.fori_loop(0, target_ref.shape[0], one, 0)


def own_kernel(grid_cols, pos_ref, own_ref, count_ref, measured_ref, object_ref, probe_ref, table_ref, *rest):
    sides = rest[:4]
    total_in, probe_total_in = rest[4:6]
    padded_ref, total_ref, probe_total_ref = rest[6:9]
    held_ref, tags_ref, patch_ref, bright_ref, rows_ref, cols_ref, sems, tag_sems, tile_sems, _ = rest[9:]
    rows, cols = object_ref.shape[1], object_ref.shape[2]
    centre = cols // LANES
    blocks = centre + 2
    tags = read_tags(side_tags(sides, rows, centre), tags_ref, tag_sems)
    tiles = start_tiles(object_ref, padded_ref, tile_sems)
    number = own_list(
        jnp.zeros((), I32), EDGE, grid_cols, rows, cols, pos_ref, own_ref, count_ref, measured_ref, held_ref, rows_ref, cols_ref, sems
    )
    for copy in tags:
        copy.wait()
    arrivals = [(ref, pattern_base(which, rows, centre), which, 0) for which, ref in enumerate(sides)]
    number = moved_list(number, False, rows, cols, arrivals, tags_ref, held_ref, rows_ref, cols_ref, sems)
    for which in (2, 3):
        down_step, _ = direction(which)
        start = pl.multiple_of(jnp.where(down_step == 1, HALF + rows, 0), HALF)
        for part in range(2):
            for block in range(centre):
                at = (part * centre + block) * HALF
                padded_ref[part * blocks + 1 + block, pl.ds(start, HALF), :] = sides[which][pl.ds(at, HALF), :]
    for which in (0, 1):
        _, right_step = direction(which)
        put_side(padded_ref, blocks, right_step == 1, pl.ds(HALF, rows), sides[which][pl.ds(0, rows), :])

    copy_planes(total_in, total_ref)
    probe_total_ref[...] = probe_total_in[...]
    for copy in tiles:
        copy.wait()
    run_pairs(number, patch_ref, bright_ref, rows_ref, cols_ref, held_ref, sems, table_ref, padded_ref, probe_ref, total_ref, probe_total_ref)


def last_kernel(grid_cols, rows, cols, pos_ref, own_ref, count_ref, measured_ref, probe_ref, table_ref, *rest):
    sides, relays = rest[:4], rest[4:6]
    padded_in, total_in, probe_total_in = rest[6:9]
    total_ref, probe_total_ref = rest[9:11]
    rim_refs = rest[11:13]
    side_refs = rest[13:15]
    padded_ref, held_ref, tags_ref, patch_ref, bright_ref, rows_ref, cols_ref, sems, tag_sems = rest[15:]
    centre = cols // LANES
    blocks = centre + 2
    last = blocks - 1
    sources = side_tags(sides, rows, centre)
    sources += [ref.at[pl.ds(RELAY_TAGS + slot * TAG_ROWS, TAG_ROWS)] for ref in relays for slot in range(2)]
    tags = read_tags(sources, tags_ref, tag_sems)
    number = own_list(
        jnp.zeros((), I32), CORNER, grid_cols, rows, cols, pos_ref, own_ref, count_ref, measured_ref, held_ref, rows_ref, cols_ref, sems
    )
    for copy in tags:
        copy.wait()
    arrivals = [(ref, pattern_base(which, rows, centre), which, 0) for which, ref in enumerate(sides)]
    number = moved_list(number, True, rows, cols, arrivals, tags_ref, held_ref, rows_ref, cols_ref, sems)
    arrivals = []
    for which, ref in enumerate(relays):
        order = jnp.where(direction(which)[1] == 1, 2, 1)
        for slot in range(2):
            arrivals.append((ref, 2 * HALF + slot * MOVE * M, 4 + 2 * which + slot, order))
    number = moved_list(number, None, rows, cols, arrivals, tags_ref, held_ref, rows_ref, cols_ref, sems)
    copy_planes(padded_in, padded_ref)
    copy_planes(total_in, total_ref)
    probe_total_ref[...] = probe_total_in[...]
    for which, ref in enumerate(relays):
        _, right_step = direction(which)
        for slot in range(2):
            down_step, _ = direction(2 + slot)
            start = pl.multiple_of(jnp.where(down_step == 1, HALF + rows, 0), HALF)
            put_side(padded_ref, blocks, right_step == 1, pl.ds(start, HALF), ref[pl.ds(slot * HALF, HALF), :])
    run_pairs(number, patch_ref, bright_ref, rows_ref, cols_ref, held_ref, sems, table_ref, padded_ref, probe_ref, total_ref, probe_total_ref)
    pack_sides(rows, centre, total_ref, side_refs)
    low = lax.broadcasted_iota(I32, (HALF, LANES), 1) < HALF
    for which, ref in zip((2, 3), rim_refs):
        down_step, _ = direction(which)
        start = pl.multiple_of(jnp.where(down_step == 1, HALF + rows, 0), HALF)
        span = pl.ds(start, HALF)
        for part in range(3):
            for block in range(centre):
                ref[pl.ds((part * centre + block) * HALF, HALF), :] = total_ref[part * blocks + 1 + block, span, :]
        at = 3 * centre * HALF
        ref[pl.ds(at, HALF), :] = jnp.where(low, pltpu.roll(total_ref[0, span, :], HALF, 1), total_ref[blocks, span, :])
        ref[pl.ds(at + HALF, HALF), :] = jnp.where(low, total_ref[last, span, :], pltpu.roll(total_ref[blocks + last, span, :], HALF, 1))
        ref[pl.ds(at + 2 * HALF, HALF), :] = jnp.where(low, total_ref[2 * blocks + last, span, :], total_ref[2 * blocks, span, :])


def pack_sides(rows, centre, total_ref, side_refs):
    blocks = centre + 2
    last = blocks - 1
    half = rows // 2
    low = lax.broadcasted_iota(I32, (rows, LANES), 1) < HALF
    low_half = lax.broadcasted_iota(I32, (half, LANES), 1) < HALF
    span = pl.ds(HALF, rows)
    for which, ref in enumerate(side_refs):
        _, right_step = direction(which)

        @pl.when(right_step == -1)
        def _():
            ref[pl.ds(0, rows), :] = jnp.where(low, pltpu.roll(total_ref[0, span, :], HALF, 1), total_ref[blocks, span, :])
            top, bottom = (total_ref[2 * blocks, pl.ds(HALF + at, half), :] for at in (0, half))
            ref[pl.ds(rows, half), :] = jnp.where(low_half, pltpu.roll(top, HALF, 1), bottom)

        @pl.when(right_step == 1)
        def _():
            ref[pl.ds(0, rows), :] = jnp.where(low, total_ref[last, span, :], pltpu.roll(total_ref[blocks + last, span, :], HALF, 1))
            top, bottom = (total_ref[2 * blocks + last, pl.ds(HALF + at, half), :] for at in (0, half))
            ref[pl.ds(rows, half), :] = jnp.where(low_half, top, pltpu.roll(bottom, HALF, 1))


def state_shapes(rows, cols):
    blocks = cols // LANES + 2
    return [
        jax.ShapeDtypeStruct((2 * blocks, rows + M, LANES), F32),
        jax.ShapeDtypeStruct((3 * blocks, rows + M, LANES), F32),
        jax.ShapeDtypeStruct((3, M, M), F32),
    ]


def list_scratch(count):
    return [pltpu.VMEM((2 * GROUP, M, M), F32), pltpu.VMEM((M, M), F32), pltpu.SMEM((count,), I32), pltpu.SMEM((count,), I32), pltpu.SemaphoreType.DMA((count,))]


def inner_patterns(scalars, measured, object_field, probe_field, tables, grid_cols):
    rows, cols = object_field.shape[1], object_field.shape[2]
    slots = measured.shape[0]
    shapes = state_shapes(rows, cols)
    return pl.pallas_call(
        lambda *refs: inner_kernel(grid_cols, *refs),
        out_shape=shapes[1:],
        in_specs=[smem_spec()] * 3 + [hbm_spec()] * 2 + [vmem_spec()] * 2,
        out_specs=[vmem_spec()] * 2,
        scratch_shapes=[pltpu.VMEM(shapes[0].shape, F32), pltpu.VMEM((slots, M, M), F32)]
        + list_scratch(slots)
        + [pltpu.SemaphoreType.DMA((2 * cols // LANES,))],
        name="inner",
        compiler_params=pltpu.CompilerParams(vmem_limit_bytes=16 << 20),
        cost_estimate=pl.CostEstimate(flops=10**10, bytes_accessed=10**7, transcendentals=0),
    )(*scalars, measured, object_field, probe_field, tables)


def own_patterns(scalars, measured, object_field, probe_field, tables, sides, state, grid_cols):
    rows, cols = object_field.shape[1], object_field.shape[2]
    centre = cols // LANES
    slots = measured.shape[0] + 4 * MOVE
    return pl.pallas_call(
        lambda *refs: own_kernel(grid_cols, *refs),
        out_shape=state_shapes(rows, cols),
        in_specs=[smem_spec()] * 3 + [hbm_spec()] * 2 + [vmem_spec()] * 8,
        out_specs=[vmem_spec()] * 3,
        scratch_shapes=[pltpu.VMEM((slots, M, M), F32), pltpu.SMEM((8, TAG_ROWS, LANES), F32)]
        + list_scratch(slots)
        + [pltpu.SemaphoreType.DMA((8,)), pltpu.SemaphoreType.DMA((2 * centre,)), pltpu.SemaphoreType.DMA((4 * centre,))],
        name="own",
        compiler_params=pltpu.CompilerParams(vmem_limit_bytes=16 << 20),
        cost_estimate=pl.CostEstimate(flops=10**10, bytes_accessed=10**7, transcendentals=0),
    )(*scalars, measured, object_field, probe_field, tables, *sides, *state)


def last_patterns(scalars, measured, probe_field, tables, sides, relays, state, rows, cols, grid_cols):
    centre = cols // LANES
    slots = measured.shape[0] + 8 * MOVE
    rim = (3 * centre + 3) * HALF
    shapes = state_shapes(rows, cols)
    return pl.pallas_call(
        lambda *refs: last_kernel(grid_cols, rows, cols, *refs),
        out_shape=shapes[1:] + [jax.ShapeDtypeStruct((rim, LANES), F32)] * 2 + [jax.ShapeDtypeStruct((rows + rows // 2, LANES), F32)] * 2,
        in_specs=[smem_spec()] * 3 + [hbm_spec()] + [vmem_spec()] * 11,
        out_specs=[vmem_spec()] * 6,
        scratch_shapes=[
            pltpu.VMEM(shapes[0].shape, F32),
            pltpu.VMEM((slots, M, M), F32),
            pltpu.SMEM((8, TAG_ROWS, LANES), F32),
        ]
        + list_scratch(slots)
        + [pltpu.SemaphoreType.DMA((8,))],
        name="last",
        compiler_params=pltpu.CompilerParams(vmem_limit_bytes=20 << 20),
        cost_estimate=pl.CostEstimate(flops=5 * 10**9, bytes_accessed=10**7, transcendentals=0),
    )(*scalars, measured, probe_field, tables, *sides, *relays, *state)


def corner_kernel(centre, first_ref, second_ref, even_ref, odd_ref):
    at = 3 * centre * HALF
    low = lax.broadcasted_iota(I32, (HALF, LANES), 1) < HALF
    lights = [ref[pl.ds(at + 2 * HALF, HALF), :] for ref in (first_ref, second_ref)]
    for which, out_ref in ((0, even_ref), (1, odd_ref)):
        _, right_step = direction(which)
        start = pl.multiple_of(at + jnp.where(right_step == 1, HALF, 0), HALF)
        out_ref[pl.ds(0, HALF), :] = first_ref[pl.ds(start, HALF), :]
        out_ref[pl.ds(HALF, HALF), :] = second_ref[pl.ds(start, HALF), :]
        keep = low == (right_step == 1)
        out_ref[pl.ds(2 * HALF, HALF), :] = jnp.where(keep, lights[0], pltpu.roll(lights[1], HALF, 1))


def corner_rims(first, second, centre):
    return pl.pallas_call(
        lambda *refs: corner_kernel(centre, *refs),
        out_shape=[jax.ShapeDtypeStruct((3 * HALF, LANES), F32)] * 2,
        in_specs=[vmem_spec()] * 2,
        out_specs=[vmem_spec()] * 2,
        name="corner",
        compiler_params=pltpu.CompilerParams(vmem_limit_bytes=4 << 20),
    )(first, second)


def final_kernel(rows, centre, object_ref, total_ref, first_ref, second_ref, even_ref, odd_ref, even_corner_ref, odd_corner_ref, out_ref, sum_ref):
    blocks = centre + 2
    half = rows // 2
    low = lax.broadcasted_iota(I32, (rows, LANES), 1) < HALF
    low_half = lax.broadcasted_iota(I32, (half, LANES), 1) < HALF
    low_corner = lax.broadcasted_iota(I32, (HALF, LANES), 1) < HALF

    def add_corners(ref, keep, from_right):
        for slot, which in enumerate((2, 3)):
            down_step, _ = direction(which)
            span = pl.ds(pl.multiple_of(jnp.where(down_step == 1, rows - HALF, 0), HALF), HALF)
            value = ref[pl.ds(slot * HALF, HALF), :]
            rolled = pltpu.roll(value, HALF, 1)
            light = ref[pl.ds(2 * HALF, HALF), :]
            if slot == 1:
                light = pltpu.roll(light, HALF, 1)
            real, imag = (rolled, value) if from_right else (value, rolled)
            for part, term in enumerate((real, imag, light)):
                sum_ref[part, span, :] += jnp.where(keep, term, 0.0)

    for block in range(centre):
        for part in range(3):
            sum_ref[part] = total_ref[part * blocks + 1 + block, pl.ds(HALF, rows), :]
            at = (part * centre + block) * HALF
            for which, ref in ((2, first_ref), (3, second_ref)):
                down_step, _ = direction(which)
                start = pl.multiple_of(jnp.where(down_step == 1, rows - HALF, 0), HALF)
                sum_ref[part, pl.ds(start, HALF), :] += ref[pl.ds(at, HALF), :]
        for which, ref, corner_ref in ((0, even_ref, even_corner_ref), (1, odd_ref, odd_corner_ref)):
            _, right_step = direction(which)
            if block == 0:

                @pl.when(right_step == -1)
                def _():
                    message = ref[pl.ds(0, rows), :]
                    sum_ref[0] += jnp.where(low, message, 0.0)
                    sum_ref[1] += jnp.where(low, pltpu.roll(message, HALF, 1), 0.0)
                    light = ref[pl.ds(rows, half), :]
                    sum_ref[2, pl.ds(0, half), :] += jnp.where(low_half, light, 0.0)
                    sum_ref[2, pl.ds(half, half), :] += jnp.where(low_half, pltpu.roll(light, HALF, 1), 0.0)
                    add_corners(corner_ref, low_corner, False)

            if block == centre - 1:

                @pl.when(right_step == 1)
                def _():
                    message = ref[pl.ds(0, rows), :]
                    sum_ref[0] += jnp.where(low, 0.0, pltpu.roll(message, HALF, 1))
                    sum_ref[1] += jnp.where(low, 0.0, message)
                    light = ref[pl.ds(rows, half), :]
                    sum_ref[2, pl.ds(0, half), :] += jnp.where(low_half, 0.0, pltpu.roll(light, HALF, 1))
                    sum_ref[2, pl.ds(half, half), :] += jnp.where(low_half, 0.0, light)
                    add_corners(corner_ref, ~low_corner, True)

        weight = 1.0 / (sum_ref[2] + FLOOR)
        lanes = pl.ds(block * LANES, LANES)
        for part in range(2):
            out_ref[part, :, lanes] = object_ref[part, :, lanes] - sum_ref[part] * weight


def finish(object_field, total, first, second, even, odd, even_corner, odd_corner, rows, centre):
    return pl.pallas_call(
        lambda *refs: final_kernel(rows, centre, *refs),
        out_shape=jax.ShapeDtypeStruct(object_field.shape, F32),
        in_specs=[vmem_spec()] * 8,
        out_specs=vmem_spec(),
        scratch_shapes=[pltpu.VMEM((3, rows, LANES), F32)],
        name="finish",
        compiler_params=pltpu.CompilerParams(vmem_limit_bytes=24 << 20),
    )(object_field, total, first, second, even, odd, even_corner, odd_corner)


def swap(block, axis, step):
    return lax.ppermute(block, axis, [(i, i ^ step) for i in range(lax.axis_size(axis))])


def halving(sizes):
    return sizes["ty"] >= 2 and not any(size & (size - 1) for size in sizes.values())


def axis_sizes():
    return {axis: lax.axis_size(axis) for axis in ("ty", "tx")}


def sum_start(value):
    if not halving(axis_sizes()):
        return value
    halves = value.reshape(2, -1, LANES)
    odd = lax.axis_index("ty") % 2
    kept = jnp.where(odd == 0, halves[0], halves[1])
    given = jnp.where(odd == 0, halves[1], halves[0])
    return kept + swap(given, "ty", 1)


def sum_finish(kept, shape):
    sizes = axis_sizes()
    if not halving(sizes):
        return lax.psum(kept, ("ty", "tx"))
    odd = lax.axis_index("ty") % 2
    if sizes["tx"] > 1:
        kept = kept + swap(kept, "tx", 1)
    for axis in ("ty", "tx"):
        step = 2
        while step < sizes[axis]:
            kept = kept + swap(kept, axis, step)
            step *= 2
    other = swap(kept, "ty", 1)
    first = jnp.where(odd == 0, kept, other)
    second = jnp.where(odd == 0, other, kept)
    return jnp.stack([first, second]).reshape(shape)


def in_vmem(values):
    return [pltpu.with_memory_space_constraint(value, pltpu.VMEM) for value in values]


def program(measured, positions, owners, counts, object_field, probe_field):
    rows, cols = object_field.shape[1], object_field.shape[2]
    centre = cols // LANES
    grid_cols = lax.axis_size("tx")
    measured = pltpu.with_memory_space_constraint(measured[0, 0], pltpu.HBM)
    tile = pltpu.with_memory_space_constraint(object_field, pltpu.HBM)
    scalars = (positions, owners, counts)
    tables = jnp.asarray(dft_blocks())
    sent = pack(scalars, measured, tile, grid_cols)
    vertical = [exchange(sent[2], 2), exchange(sent[3], 3)]
    sides = [exchange(sent[0], 0), exchange(sent[1], 1)] + vertical
    inner = in_vmem(inner_patterns(scalars, measured, tile, probe_field, tables, grid_cols))
    relays = relay(*vertical, centre)
    relays = [exchange(relays[0], 0), exchange(relays[1], 1)]
    state = in_vmem(own_patterns(scalars, measured, tile, probe_field, tables, sides, inner, grid_cols))
    total, probe_total, rim_even, rim_odd, side_even, side_odd = last_patterns(
        scalars, measured, probe_field, tables, sides, relays, state, rows, cols, grid_cols
    )
    (total,) = in_vmem([total])
    kept = sum_start(probe_total)
    rim_even = exchange(rim_even, 2)
    rim_odd = exchange(rim_odd, 3)
    side_even = exchange(side_even, 0)
    side_odd = exchange(side_odd, 1)
    corner_even, corner_odd = corner_rims(rim_even, rim_odd, centre)
    corner_even = exchange(corner_even, 0)
    corner_odd = exchange(corner_odd, 1)
    new_object = finish(object_field, total, rim_even, rim_odd, side_even, side_odd, corner_even, corner_odd, rows, centre)
    summed = sum_finish(kept, probe_total.shape)
    new_probe = probe_field - summed[:2] / (summed[2] + TINY)
    return new_object, new_probe


def solution(mesh):
    placed = (
        P("ty", "tx", None, None, None),
        P("ty", "tx", None, None),
        P("ty", "tx", None),
        P("ty", "tx"),
        P(None, "ty", "tx"),
        P(),
    )
    return jax.shard_map(program, mesh=mesh, in_specs=placed, out_specs=(P(None, "ty", "tx"), P()), check_vma=False)
```
